32 devices in a mesh: grp: 2 (over x), tpl: 16 (over z, y, core).
Axes of the slice: x: 2, y: 2, z: 4, core: 2. Of those that a mesh axis runs over, the one named last changes fastest.
Arguments:
- strain_slots: bfloat16 [32, 3, 2, 262144], P(('grp', 'tpl')), parts along dimension 0, may hold values from -6 to 6
- templates: bfloat16 [32, 2, 262144], P(None, None, 'tpl'), may hold values from -6 to 6
- cutoffs: int32 [32], replicated, may hold values from 32768 to 262144
- lists: int32 [16, 2], replicated, may hold values from 0 to 31, as said below
- owner: int32 [2], P('grp'), parts along dimension 0, may hold values from 0 to 15
- slides: int32 [6], P('grp'), parts along dimension 0, may hold values from 0 to 262143
Outputs:
- peaks: float32 [64], P(('grp', 'tpl')), parts along dimension 0
- norms: float32 [64], P(('grp', 'tpl')), parts along dimension 0
The draws below stay inside these ranges and needn't reach their ends.
There are 2 independent parts, one for each index of `grp`. The reference program is written for one: setup_inputs(seed, part) draws one part's arguments, and reference() takes and returns one part's arrays. A program takes and returns all parts, laid end to end along the dimension named above; an argument that names none is the same for every part. Nothing has to cross between parts.
Inputs may be any that keep to these rules, and one draw needn't show every extreme that they name: Every template appears once in lists; list positions in row-major order run through the templates by falling cutoffs. One template has cutoff 262144, one has 32768.
All inputs are finite; a program needn't handle non-finite values.
Results may differ from the reference program's by a relative error of at most 0.0021.
Values may be sent and summed in bfloat16 or wider, within the bound.
A program may use at most 128 MiB of HBM per device.

```python
import jax
import jax.numpy as jnp
from jax import lax

DET = 3
ROWS = 512
COLS = 512
TPL_DEV = 2
BINS = 262144
TEMPLATES = 32
SLOTS = 16
N_TPL = 16


def bank_draw(key):
    keys = jax.random.split(jax.random.fold_in(key, 7), 3)
    cutoff_bins = jax.random.randint(keys[0], (TEMPLATES,), BINS // 8, BINS + 1)
    marks = jax.random.permutation(keys[1], TEMPLATES)
    cutoff_bins = jnp.where(marks == 0, BINS, cutoff_bins)
    cutoff_bins = jnp.where(marks == 1, BINS // 8, cutoff_bins)
    breakers = jax.random.permutation(keys[2], TEMPLATES)
    scores = cutoff_bins * TEMPLATES + breakers
    ordered = jnp.argsort(-scores, stable=True)
    return (cutoff_bins.astype(jnp.int32), ordered.astype(jnp.int32).reshape(TEMPLATES // TPL_DEV, TPL_DEV))


def draw_cutoffs(key, part):
    return bank_draw(key)[0]


def draw_lists(key, part):
    return bank_draw(key)[1]


def level_of(rng, shape, cuts, least, largest):
    factor_of, own = 1.0, jax.random.fold_in(rng, 6)
    for axis_at, parts in cuts:
        draws = jnp.exp(jax.random.uniform(jax.random.fold_in(own, axis_at), (parts,), jnp.float32, least / len(cuts), largest / len(cuts)))
        factor_of = factor_of * jnp.repeat(draws, shape[axis_at] // parts).reshape([-1 if axis == axis_at else 1 for axis in range(len(shape))])
    return factor_of


def normal_values(key, shape, scale, bound, shards=(), held_as=jnp.bfloat16):
    level = level_of(key, shape, shards, -0.22, 0.18) if shards else 1.0
    result = jax.random.normal(key, shape, jnp.float32) * scale * level
    return jnp.minimum(jnp.maximum(result, -bound), bound).astype(held_as)


def setup_inputs(seed: int = 0, part: int = 0) -> dict:
    key_list = jax.random.split(jax.random.key(seed), 7)
    part_splits = jax.random.split(jax.random.fold_in(key_list[6], part), 7)
    return {
        "strain_slots": normal_values(part_splits[0], (SLOTS, DET, 2, BINS), 1.0, 6.0, ((0, 16),)),
        "templates": normal_values(key_list[1], (TEMPLATES, 2, BINS), 1.0, 6.0, ((2, 16),)),
        "cutoffs": draw_cutoffs(jax.random.fold_in(key_list[6], 71), part),
        "lists": draw_lists(jax.random.fold_in(key_list[6], 71), part),
        "owner": jax.random.randint(part_splits[4], (1,), 0, N_TPL).astype(jnp.int32),
        "slides": jax.random.randint(part_splits[5], (DET,), 0, BINS).astype(jnp.int32),
    }


two_pi = 6.283185307179586
eps_norm = 1e-6


def turn_table(left_ids, right_ids, period):
    product_idx = (left_ids[:, None] * right_ids[None, :]) % period
    angles = product_idx.astype(jnp.float32) * (two_pi / period)
    return jnp.cos(angles), jnp.sin(angles)


def slide_phases(slides):
    total = ROWS * COLS
    bin_ids = jnp.arange(total, dtype=jnp.int32)
    row_ids = bin_ids // COLS
    col_ids = bin_ids % COLS
    stride = (COLS * slides) % total
    turns = ((row_ids[None, :] * stride[:, None]) % total + (col_ids[None, :] * slides[:, None]) % total) % total
    angles = turns.astype(jnp.float32) * (two_pi / total)
    return jnp.cos(angles), jnp.sin(angles)


def rounded(values):
    return lax.optimization_barrier(values.astype(jnp.bfloat16)).astype(jnp.float32)


def reference(strain_slots, templates, cutoffs, lists, owner, slides):
    total = ROWS * COLS
    strain = lax.dynamic_index_in_dim(strain_slots, owner[0], 0, keepdims=False).astype(jnp.float32)
    row_ids = jnp.arange(ROWS, dtype=jnp.int32)
    col_ids = jnp.arange(COLS, dtype=jnp.int32)
    row_cos, row_sin = turn_table(row_ids, row_ids, ROWS)
    row_table = rounded(jnp.concatenate([jnp.concatenate([row_cos, -row_sin], 1), jnp.concatenate([row_sin, row_cos], 1)], 0))
    twiddle_cos, twiddle_sin = turn_table(row_ids, col_ids, total)
    col_cos, col_sin = turn_table(col_ids, col_ids, COLS)
    col_table = rounded(jnp.concatenate([jnp.concatenate([col_cos, col_sin], 1), jnp.concatenate([-col_sin, col_cos], 1)], 0))
    phase_cos, phase_sin = slide_phases(slides)
    data_re = strain[:, 0]
    data_im = strain[:, 1]

    def filter_one(template_id):
        waveform = lax.dynamic_index_in_dim(templates, template_id, 0, keepdims=False).astype(jnp.float32)
        cutoff = lax.dynamic_index_in_dim(cutoffs, template_id, 0, keepdims=False)
        inside = jnp.arange(total, dtype=jnp.int32) < cutoff
        wave_re = waveform[0]
        wave_im = waveform[1]
        real_part = data_re * wave_re + data_im * wave_im
        imag_part = data_im * wave_re - data_re * wave_im
        prod_re = jnp.where(inside, real_part * phase_cos - imag_part * phase_sin, jnp.float32(0.0))
        prod_im = jnp.where(inside, real_part * phase_sin + imag_part * phase_cos, jnp.float32(0.0))
        stacked = rounded(jnp.concatenate([prod_re.reshape(DET, ROWS, COLS), prod_im.reshape(DET, ROWS, COLS)], 1))
        section_one = jnp.einsum("ab,dbc->dac", row_table, stacked, precision=lax.Precision.HIGHEST)
        first_re = section_one[:, :ROWS]
        first_im = section_one[:, ROWS:]
        twisted = rounded(jnp.concatenate([first_re * twiddle_cos - first_im * twiddle_sin, first_re * twiddle_sin + first_im * twiddle_cos], 2))
        series = jnp.einsum("dab,bc->dac", twisted, col_table, precision=lax.Precision.HIGHEST)
        series_re = series[:, :, :COLS]
        series_im = series[:, :, COLS:]
        power_sum = jnp.sum(series_re * series_re + series_im * series_im, axis=0)
        sigmasq = jnp.sum(jnp.where(inside, wave_re * wave_re + wave_im * wave_im, jnp.float32(0.0)))
        return jnp.max(power_sum) / (2.0 * (sigmasq + eps_norm)), sigmasq / total

    peaks, norms = lax.map(filter_one, lists.reshape(-1).astype(jnp.int32))
    return peaks, norms
```

```python
import functools

import jax
import jax.numpy as jnp
import numpy as np
from jax import lax
from jax.experimental import pallas as pl
from jax.experimental.pallas import tpu as pltpu
from jax.sharding import PartitionSpec as P

ROWS = 512
COLS = 512
RADIX = 4
FOLD = ROWS // RADIX
WIDE = RADIX * COLS
HALF = COLS // 2

two_pi = 6.283185307179586
eps_norm = 1e-06


def turn_table(left_ids, right_ids, period):
    product_idx = left_ids[:, None] * right_ids[None, :] % period
    angles = product_idx.astype(np.float32) * np.float32(two_pi / period)
    return np.cos(angles), np.sin(angles)


def constant_tables():
    ids = np.arange(ROWS, dtype=np.int32)
    cos, sin = turn_table(ids[:FOLD], ids, ROWS)
    first = []
    for r in range(RADIX):
        c, s = cos[:, r::RADIX], sin[:, r::RADIX]
        first.append(np.concatenate([np.concatenate([c, -s], 1), np.concatenate([s, c], 1)], 0))
    twiddle = np.stack(turn_table(ids, ids, ROWS * COLS))
    cos, sin = turn_table(ids, ids[: HALF + 1], COLS)
    sin = sin[:, :HALF].copy()
    sin[:, 0] = cos[:, HALF]
    second = np.concatenate([cos[:, :HALF], sin], 1)
    return np.stack(first).astype(jnp.bfloat16), twiddle, second.astype(jnp.bfloat16)


def filter_kernel(
    cutoffs, strain, wave, row_phase, col_phase, first, twiddle, second,
    peaks, norms, turned, masked, twisted, total_q, total_r,
):
    dets = strain.shape[0]
    templates = wave.shape[0]
    bins = ROWS * COLS

    def turn(i, _):
        d, rows = i // 8, pl.ds(pl.multiple_of(i % 8 * 16, 16), 16)
        for c in range(WIDE // 512):
            cols = pl.ds(c * 512, 512)
            rr = jnp.concatenate([row_phase[d, 0, rows, :]] * 4, 1)
            ri = jnp.concatenate([row_phase[d, 1, rows, :]] * 4, 1)
            cr, ci = col_phase[d, 0, :, cols], col_phase[d, 1, :, cols]
            pr, pi = rr * cr - ri * ci, rr * ci + ri * cr
            xr = strain[d, 0, rows, cols].astype(jnp.float32)
            xi = strain[d, 1, rows, cols].astype(jnp.float32)
            turned[d, 0, rows, cols] = xr * pr - xi * pi
            turned[d, 1, rows, cols] = xr * pi + xi * pr
        return 0

    lax.fori_loop(0, dets * 8, turn, 0)

    def one_template(t, _):
        cutoff = cutoffs[t]

        def mask(i, acc):
            rows = pl.ds(pl.multiple_of(i * 16, 16), 16)
            for c in range(WIDE // 512):
                cols = pl.ds(c * 512, 512)
                at = (
                    lax.broadcasted_iota(jnp.int32, (16, 512), 0) + i * 16
                ) * WIDE + lax.broadcasted_iota(jnp.int32, (16, 512), 1) + c * 512
                inside = at < cutoff
                wr = jnp.where(inside, wave[t, 0, rows, cols].astype(jnp.float32), 0.0)
                wi = jnp.where(inside, wave[t, 1, rows, cols].astype(jnp.float32), 0.0)
                masked[0, rows, cols] = wr
                masked[1, rows, cols] = wi
                acc = acc + (wr * wr + wi * wi)
            return acc

        acc = lax.fori_loop(0, FOLD // 16, mask, jnp.zeros((16, 512), jnp.float32))
        sigmasq = jnp.sum(acc)

        def one_detector(d, _):
            for c in range(COLS // 256):
                parts = []
                for r in range(RADIX):
                    cols = pl.ds(r * COLS + c * 256, 256)
                    xr, xi = turned[d, 0, :, cols], turned[d, 1, :, cols]
                    wr, wi = masked[0, :, cols], masked[1, :, cols]
                    product = jnp.concatenate([xr * wr + xi * wi, xi * wr - xr * wi], 0)
                    out = jnp.dot(
                        first[r], product.astype(jnp.bfloat16), preferred_element_type=jnp.float32
                    )
                    parts.append((out[:FOLD], out[FOLD:]))
                (r0, i0), (r1, i1), (r2, i2), (r3, i3) = parts
                ar, ai, br, bi = r0 + r2, i0 + i2, r0 - r2, i0 - i2
                cr, ci, dr, di = r1 + r3, i1 + i3, i3 - i1, r1 - r3
                sections = (
                    (ar + cr, ai + ci), (br + dr, bi + di), (ar - cr, ai - ci), (br - dr, bi - di)
                )
                cols = pl.ds(c * 256, 256)
                for q, (sr, si) in enumerate(sections):
                    rows = pl.ds(q * FOLD, FOLD)
                    tc, ts = twiddle[0, rows, cols], twiddle[1, rows, cols]
                    twisted[0, rows, cols] = (sr * tc - si * ts).astype(jnp.bfloat16)
                    twisted[1, rows, cols] = (sr * ts + si * tc).astype(jnp.bfloat16)
            for q in range(RADIX):
                rows = pl.ds(q * FOLD, FOLD)
                ac = jnp.dot(twisted[0, rows, :], second[...], preferred_element_type=jnp.float32)
                db = jnp.dot(twisted[1, rows, :], second[...], preferred_element_type=jnp.float32)
                a, c, dd, b = ac[:, :HALF], ac[:, HALF:], db[:, :HALF], db[:, HALF:]
                ad, bc = a * a + dd * dd, b * b + c * c
                both = ad + bc
                cross = 2.0 * (c * dd - a * b)
                lane = lax.broadcasted_iota(jnp.int32, both.shape, 1)
                edge = lane == 0
                both, cross = jnp.where(edge, 0.5 * both, both), jnp.where(edge, 0.5 * (ad - bc), cross)

                @pl.when(d == 0)
                def _():
                    total_q[rows, :] = both
                    total_r[rows, :] = cross

                @pl.when(d > 0)
                def _():
                    total_q[rows, :] += both
                    total_r[rows, :] += cross
            return 0

        lax.fori_loop(0, dets, one_detector, 0)

        def largest(i, acc):
            rows = pl.ds(pl.multiple_of(i * 32, 32), 32)
            return jnp.maximum(acc, total_q[rows, :] + jnp.abs(total_r[rows, :]))

        best = lax.fori_loop(0, ROWS // 32, largest, jnp.zeros((32, HALF), jnp.float32))
        peaks[t] = jnp.max(best) / (2.0 * (sigmasq + eps_norm))
        norms[t] = sigmasq / bins
        return 0

    lax.fori_loop(0, templates, one_template, 0)


def run_filter(cutoffs, strain, wave, row_phase, col_phase):
    templates, dets = wave.shape[0], strain.shape[0]
    first, twiddle, second = constant_tables()
    vmem = pl.BlockSpec(memory_space=pltpu.VMEM)
    smem = pl.BlockSpec(memory_space=pltpu.SMEM)
    out = jax.ShapeDtypeStruct((templates,), jnp.float32)
    return pl.pallas_call(
        filter_kernel,
        out_shape=(out, out),
        in_specs=[smem] + [vmem] * 7,
        out_specs=(smem, smem),
        scratch_shapes=[
            pltpu.VMEM((dets, 2, FOLD, WIDE), jnp.float32),
            pltpu.VMEM((2, FOLD, WIDE), jnp.float32),
            pltpu.VMEM((2, ROWS, COLS), jnp.bfloat16),
            pltpu.VMEM((ROWS, HALF), jnp.float32),
            pltpu.VMEM((ROWS, HALF), jnp.float32),
        ],
        compiler_params=pltpu.CompilerParams(vmem_limit_bytes=56 * 1024 * 1024),
        name="filter",
    )(cutoffs, strain, wave, row_phase, col_phase, jnp.asarray(first), jnp.asarray(twiddle), jnp.asarray(second))


def phases(slides):
    total = ROWS * COLS
    slides = slides[:, None]
    row = jnp.arange(FOLD, dtype=jnp.int32)[None] * slides % FOLD
    col = jnp.arange(WIDE, dtype=jnp.int32)[None] * slides % total
    row = row.astype(jnp.float32) * (two_pi / FOLD)
    col = col.astype(jnp.float32) * (two_pi / total)
    row = jnp.stack([jnp.cos(row), jnp.sin(row)], 1)
    col = jnp.stack([jnp.cos(col), jnp.sin(col)], 1)
    return jnp.broadcast_to(row[..., None], row.shape + (128,)), col[:, :, None, :]


def body(strain_slots, templates, cutoffs, lists, owner, slides):
    devices = lax.axis_size("tpl")
    own_index = lax.axis_index("tpl")
    per_device = lists.shape[1]
    chosen = lists.reshape(-1)
    dets = strain_slots.shape[1]
    strain = strain_slots[0].reshape(dets, 2, FOLD, WIDE)
    strain = jnp.where(own_index == owner[0], strain, jnp.zeros_like(strain))
    strain = lax.psum(strain, "tpl")
    rows = templates.shape[2] // WIDE
    picked = templates[chosen].reshape(devices, per_device, 2, rows, WIDE)
    arrived = lax.all_to_all(picked, "tpl", split_axis=0, concat_axis=3, tiled=True)[0]
    own_ids = lax.dynamic_index_in_dim(lists, own_index, 0, keepdims=False)
    row_phase, col_phase = phases(slides)
    return run_filter(cutoffs[own_ids], strain, arrived, row_phase, col_phase)


def solution(mesh):
    in_specs = (
        P(("grp", "tpl"), None, None, None),
        P(None, None, "tpl"),
        P(),
        P(),
        P("grp"),
        P("grp"),
    )
    out_specs = (P(("grp", "tpl")), P(("grp", "tpl")))
    return jax.shard_map(body, mesh=mesh, in_specs=in_specs, out_specs=out_specs, check_vma=False)
```

```python
import functools

import jax
import jax.numpy as jnp
import numpy as np
from jax import lax
from jax.experimental import pallas as pl
from jax.experimental.pallas import tpu as pltpu
from jax.sharding import PartitionSpec as P

ROWS = 512
COLS = 512
RADIX = 4
FOLD = ROWS // RADIX
WIDE = RADIX * COLS
HALF = COLS // 2

two_pi = 6.283185307179586
eps_norm = 1e-06


def turn_table(left_ids, right_ids, period):
    product_idx = left_ids[:, None] * right_ids[None, :] % period
    angles = product_idx.astype(np.float32) * np.float32(two_pi / period)
    return np.cos(angles), np.sin(angles)


def constant_tables():
    ids = np.arange(ROWS, dtype=np.int32)
    cos, sin = turn_table(ids[:FOLD], ids, ROWS)
    first = []
    for r in range(RADIX):
        c, s = cos[:, r::RADIX], sin[:, r::RADIX]
        first.append(np.concatenate([np.concatenate([c, -s], 1), np.concatenate([s, c], 1)], 0))
    twiddle = np.stack(turn_table(ids, ids, ROWS * COLS))
    cos, sin = turn_table(ids, ids[: HALF + 1], COLS)
    sin = sin[:, :HALF].copy()
    sin[:, 0] = cos[:, HALF]
    second = np.concatenate([cos[:, :HALF], sin], 1)
    return np.stack(first).astype(jnp.bfloat16), twiddle, second.astype(jnp.bfloat16)


def filter_kernel(
    cutoffs, strain, wave, row_phase, col_phase, first, twiddle, second,
    peaks, norms, turned, masked, twisted, total_q, total_r,
):
    dets = strain.shape[0]
    templates = wave.shape[0]
    bins = ROWS * COLS

    def turn(i, _):
        d, rows = i // 8, pl.ds(pl.multiple_of(i % 8 * 16, 16), 16)
        for c in range(WIDE // 512):
            cols = pl.ds(c * 512, 512)
            rr = jnp.concatenate([row_phase[d, 0, rows, :]] * 4, 1)
            ri = jnp.concatenate([row_phase[d, 1, rows, :]] * 4, 1)
            cr, ci = col_phase[d, 0, :, cols], col_phase[d, 1, :, cols]
            pr, pi = rr * cr - ri * ci, rr * ci + ri * cr
            xr = strain[d, 0, rows, cols].astype(jnp.float32)
            xi = strain[d, 1, rows, cols].astype(jnp.float32)
            turned[d, 0, rows, cols] = xr * pr - xi * pi
            turned[d, 1, rows, cols] = xr * pi + xi * pr
        return 0

    lax.fori_loop(0, dets * 8, turn, 0)

    def one_template(t, _):
        cutoff = cutoffs[t]

        blocks = 8 // wave.shape[3]

        def mask(i, acc):
            rows = pl.ds(pl.multiple_of(i * 8, 8), 8)
            for c in range(WIDE // 512):
                cols = pl.ds(c * 512, 512)
                at = (
                    lax.broadcasted_iota(jnp.int32, (8, 512), 0) + i * 8
                ) * WIDE + lax.broadcasted_iota(jnp.int32, (8, 512), 1) + c * 512
                inside = at < cutoff
                parts = []
                for p in range(2):
                    got = [
                        wave[t, p, i * blocks + e, :, cols].astype(jnp.float32) for e in range(blocks)
                    ]
                    got = got[0] if blocks == 1 else jnp.concatenate(got, 0)
                    parts.append(jnp.where(inside, got, 0.0))
                    masked[p, rows, cols] = parts[p]
                acc = acc + (parts[0] * parts[0] + parts[1] * parts[1])
            return acc

        acc = lax.fori_loop(0, FOLD // 8, mask, jnp.zeros((8, 512), jnp.float32))
        sigmasq = jnp.sum(acc)

        def one_detector(d, _):
            for c in range(COLS // 256):
                parts = []
                for r in range(RADIX):
                    cols = pl.ds(r * COLS + c * 256, 256)
                    xr, xi = turned[d, 0, :, cols], turned[d, 1, :, cols]
                    wr, wi = masked[0, :, cols], masked[1, :, cols]
                    product = jnp.concatenate([xr * wr + xi * wi, xi * wr - xr * wi], 0)
                    out = jnp.dot(
                        first[r], product.astype(jnp.bfloat16), preferred_element_type=jnp.float32
                    )
                    parts.append((out[:FOLD], out[FOLD:]))
                (r0, i0), (r1, i1), (r2, i2), (r3, i3) = parts
                ar, ai, br, bi = r0 + r2, i0 + i2, r0 - r2, i0 - i2
                cr, ci, dr, di = r1 + r3, i1 + i3, i3 - i1, r1 - r3
                sections = (
                    (ar + cr, ai + ci), (br + dr, bi + di), (ar - cr, ai - ci), (br - dr, bi - di)
                )
                cols = pl.ds(c * 256, 256)
                for q, (sr, si) in enumerate(sections):
                    rows = pl.ds(q * FOLD, FOLD)
                    tc, ts = twiddle[0, rows, cols], twiddle[1, rows, cols]
                    twisted[0, rows, cols] = (sr * tc - si * ts).astype(jnp.bfloat16)
                    twisted[1, rows, cols] = (sr * ts + si * tc).astype(jnp.bfloat16)
            for q in range(RADIX):
                rows = pl.ds(q * FOLD, FOLD)
                ac = jnp.dot(twisted[0, rows, :], second[...], preferred_element_type=jnp.float32)
                db = jnp.dot(twisted[1, rows, :], second[...], preferred_element_type=jnp.float32)
                a, c, dd, b = ac[:, :HALF], ac[:, HALF:], db[:, :HALF], db[:, HALF:]
                ad, bc = a * a + dd * dd, b * b + c * c
                both = ad + bc
                cross = 2.0 * (c * dd - a * b)
                lane = lax.broadcasted_iota(jnp.int32, both.shape, 1)
                edge = lane == 0
                both, cross = jnp.where(edge, 0.5 * both, both), jnp.where(edge, 0.5 * (ad - bc), cross)

                @pl.when(d == 0)
                def _():
                    total_q[rows, :] = both
                    total_r[rows, :] = cross

                @pl.when(d > 0)
                def _():
                    total_q[rows, :] += both
                    total_r[rows, :] += cross
            return 0

        lax.fori_loop(0, dets, one_detector, 0)

        def largest(i, acc):
            rows = pl.ds(pl.multiple_of(i * 32, 32), 32)
            return jnp.maximum(acc, total_q[rows, :] + jnp.abs(total_r[rows, :]))

        best = lax.fori_loop(0, ROWS // 32, largest, jnp.zeros((32, HALF), jnp.float32))
        peaks[t] = jnp.max(best) / (2.0 * (sigmasq + eps_norm))
        norms[t] = sigmasq / bins
        return 0

    lax.fori_loop(0, templates, one_template, 0)


def run_filter(cutoffs, strain, wave, row_phase, col_phase):
    templates, dets = wave.shape[0], strain.shape[0]
    first, twiddle, second = constant_tables()
    vmem = pl.BlockSpec(memory_space=pltpu.VMEM)
    smem = pl.BlockSpec(memory_space=pltpu.SMEM)
    out = jax.ShapeDtypeStruct((templates,), jnp.float32)
    return pl.pallas_call(
        filter_kernel,
        out_shape=(out, out),
        in_specs=[smem] + [vmem] * 7,
        out_specs=(smem, smem),
        scratch_shapes=[
            pltpu.VMEM((dets, 2, FOLD, WIDE), jnp.float32),
            pltpu.VMEM((2, FOLD, WIDE), jnp.float32),
            pltpu.VMEM((2, ROWS, COLS), jnp.bfloat16),
            pltpu.VMEM((ROWS, HALF), jnp.float32),
            pltpu.VMEM((ROWS, HALF), jnp.float32),
        ],
        compiler_params=pltpu.CompilerParams(vmem_limit_bytes=56 * 1024 * 1024),
        name="filter",
    )(cutoffs, strain, wave, row_phase, col_phase, jnp.asarray(first), jnp.asarray(twiddle), jnp.asarray(second))


def phases(slides):
    total = ROWS * COLS
    slides = slides[:, None]
    row = jnp.arange(FOLD, dtype=jnp.int32)[None] * slides % FOLD
    col = jnp.arange(WIDE, dtype=jnp.int32)[None] * slides % total
    row = row.astype(jnp.float32) * (two_pi / FOLD)
    col = col.astype(jnp.float32) * (two_pi / total)
    row = jnp.stack([jnp.cos(row), jnp.sin(row)], 1)
    col = jnp.stack([jnp.cos(col), jnp.sin(col)], 1)
    return jnp.broadcast_to(row[..., None], row.shape + (128,)), col[:, :, None, :]


MESH = pl.DeviceIdType.MESH


def share_kernel(
    width_y, flags, strain, picked, full, arrived, other, ring_in, first_out,
    core_send, core_recv, sum_send, sum_recv, all_send, all_recv, part_send, part_recv,
    swap_send, swap_recv, own_sem, cross_send, cross_recv,
):
    n, groups = lax.axis_size("tpl"), lax.axis_size("grp")
    me, group = lax.axis_index("tpl"), lax.axis_index("grp")
    chips = n // 2
    core, chip = me % 2, me // 2
    depth = chips // width_y
    y, z = chip % width_y, chip // width_y
    pos = z + y * (2 * depth - 1 - 2 * z)
    half = strain.shape[1] // 2
    prow, pcol = ring_in.shape[3], ring_in.shape[4]
    colparts = strain.shape[2] // pcol
    subs = strain.shape[0] // 2
    share = arrived.shape[0] // groups
    mine = pl.ds(group * share, share)
    partner = me + 1 - 2 * core

    def device_at(p):
        p = (p + chips) % chips
        yy = p // depth
        zz = p + yy * (2 * depth - 1 - 2 * p)
        return (zz * width_y + yy) * 2 + core

    nexts = (device_at(pos + 1), device_at(pos - 1))

    def chunk(direction, back):
        return (pos - back + 2 * chips) % chips if direction == 0 else (pos + back) % chips

    def spot(base, j):
        rows = pl.multiple_of(base + j // colparts * prow, prow)
        return pl.ds(rows, prow), pl.ds(pl.multiple_of(j % colparts * pcol, pcol), pcol)

    def piece(ref, base, direction, k, j):
        return ref.at[(direction * subs + k,) + spot(base, j)]

    def remote(src, dst, send, recv, **where):
        return pltpu.make_async_remote_copy(
            src_ref=src, dst_ref=dst, send_sem=send, recv_sem=recv,
            device_id=where, device_id_type=MESH,
        )

    def core_copy(direction, back):
        j = chunk(direction, back)
        planes = pl.ds(direction * subs, subs)
        return remote(
            strain.at[(planes,) + spot((1 - core) * half, j)],
            other.at[(planes,) + spot(0, j)],
            core_send.at[back, direction], core_recv.at[back, direction], tpl=partner,
        )

    def sum_copy(direction, k, s):
        src = first_out.at[direction, k]
        if not isinstance(s, int):
            src = ring_in.at[s - 1, direction, k]
        return remote(
            src, ring_in.at[s, direction, k],
            sum_send.at[s, direction, k], sum_recv.at[s, direction, k], tpl=nexts[direction],
        )

    def all_copy(direction, k, s):
        at = piece(full, core * half, direction, k, chunk(direction, s))
        return remote(
            at, at, all_send.at[s, direction, k], all_recv.at[s, direction, k], tpl=nexts[direction]
        )

    def part_copy(direction, k, s, base):
        at = piece(full, base, direction, k, chunk(direction, s))
        return remote(
            at, at, part_send.at[s, direction, k], part_recv.at[s, direction, k], tpl=partner
        )

    def swap_copy(i):
        to = (me - i + n) % n
        return remote(
            picked.at[to, mine], arrived.at[mine, me], swap_send.at[i], swap_recv.at[i], tpl=to
        )

    def swap_arrival(i):
        source = (me + i) % n
        return remote(
            picked.at[me, mine], arrived.at[mine, source], swap_send.at[i], swap_recv.at[i], tpl=source
        )

    def cross_copy(i, g):
        at = arrived.at[mine, (me + i) % n]
        return remote(
            at, at, cross_send.at[g - 1, i], cross_recv.at[g - 1, i], grp=(group + g) % groups
        )

    def cross_arrival(i, g):
        source = (group - g + groups) % groups
        at = arrived.at[pl.ds(source * share, share), (me + i) % n]
        return remote(at, at, cross_send.at[g - 1, i], cross_recv.at[g - 1, i], grp=source)

    barrier = pltpu.get_barrier_semaphore()

    def greet(i, _):
        pl.semaphore_signal(barrier, inc=1, device_id={"tpl": (me + i) % n}, device_id_type=MESH)
        return 0

    lax.fori_loop(1, n, greet, 0)
    for g in range(1, groups):
        pl.semaphore_signal(
            barrier, inc=1, device_id={"grp": (group + g) % groups}, device_id_type=MESH
        )
    pl.semaphore_wait(barrier, n - 1 + groups - 1)

    own = pltpu.make_async_copy(picked.at[me], arrived.at[:, me], own_sem)
    own.start()

    def start_core(i, _):
        for direction in range(2):
            core_copy(direction, i + 1 - (i + 1) // chips * chips).start()
        return 0

    lax.fori_loop(0, chips, start_core, 0)
    i_own, chip_owns = flags[0], flags[1]

    def candidate(direction, k, j):
        here = piece(strain, core * half, direction, k, j)[...]
        there = piece(other, 0, direction, k, j)[...]
        return jnp.where(i_own != 0, here, there)

    for direction in range(2):
        core_copy(direction, 1).wait_recv()
        for k in range(subs):
            first_out[direction, k] = candidate(direction, k, chunk(direction, 1))
            sum_copy(direction, k, 0).start()

    def start_swap(i, _):
        swap_copy(i).start()
        return 0

    lax.fori_loop(1, n, start_swap, 0)

    def joined(direction, k, s, j):
        remote(
            first_out.at[direction, k], ring_in.at[s, direction, k],
            sum_send.at[s, direction, k], sum_recv.at[s, direction, k], tpl=nexts[direction],
        ).wait_recv()
        return jnp.where(chip_owns != 0, candidate(direction, k, j), ring_in[s, direction, k])

    def sum_step(s, _):
        for direction in range(2):
            core_copy(direction, s + 2).wait_recv()
        for k in range(subs):
            for direction in range(2):
                ring_in[s, direction, k] = joined(direction, k, s, chunk(direction, s + 2))
                sum_copy(direction, k, s + 1).start()
        return 0

    lax.fori_loop(0, chips - 2, sum_step, 0)
    for direction in range(2):
        core_copy(direction, 0).wait_recv()
    for k in range(subs):
        for direction in range(2):
            piece(full, core * half, direction, k, pos)[...] = joined(direction, k, chips - 2, pos)
            all_copy(direction, k, 0).start()
            part_copy(direction, k, 0, core * half).start()

    def cross_start(i):
        swap_arrival(i).wait_recv()
        for g in range(1, groups):
            cross_copy(i, g).start()

    per_step = (n - 1) // (chips - 1)

    def all_step(s, _):
        for k in range(subs):
            for direction in range(2):
                at = piece(full, core * half, direction, k, chunk(direction, s + 1))
                remote(
                    at, at, all_send.at[s, direction, k], all_recv.at[s, direction, k],
                    tpl=nexts[direction],
                ).wait_recv()
                all_copy(direction, k, s + 1).start()
                part_copy(direction, k, s + 1, core * half).start()
        for e in range(per_step):
            cross_start(1 + s * per_step + e)
        return 0

    lax.fori_loop(0, chips - 2, all_step, 0)
    last = chips - 2
    for k in range(subs):
        for direction in range(2):
            at = piece(full, core * half, direction, k, chunk(direction, last + 1))
            remote(
                at, at, all_send.at[last, direction, k], all_recv.at[last, direction, k],
                tpl=nexts[direction],
            ).wait_recv()
            part_copy(direction, k, last + 1, core * half).start()
    for i in range(1 + last * per_step, n):
        cross_start(i)

    def finish(s, _):
        for direction in range(2):
            core_copy(direction, s).wait_send()
            for k in range(subs):
                part_copy(direction, k, s, core * half).wait_send()
                part_copy(direction, k, s, (1 - core) * half).wait_recv()
        return 0

    lax.fori_loop(0, chips, finish, 0)

    def finish_ring(s, _):
        for direction in range(2):
            for k in range(subs):
                all_copy(direction, k, s).wait_send()
                remote(
                    first_out.at[direction, k], ring_in.at[s, direction, k],
                    sum_send.at[s, direction, k], sum_recv.at[s, direction, k], tpl=nexts[direction],
                ).wait_send()
        return 0

    lax.fori_loop(0, chips - 1, finish_ring, 0)

    def finish_swap(i, _):
        swap_copy(i).wait_send()
        for g in range(1, groups):
            cross_copy(i, g).wait_send()
            cross_arrival(i, g).wait_recv()
        return 0

    lax.fori_loop(1, n, finish_swap, 0)
    own.wait()


def run_share(width_y, flags, strain, picked):
    n, groups = lax.axis_size("tpl"), lax.axis_size("grp")
    chips = n // 2
    planes, high, wide = strain.shape
    subs = planes // 2
    rowparts = max(1, chips * 256 // wide)
    prow, pcol = high // 2 // rowparts, wide * rowparts // chips
    vmem = pl.BlockSpec(memory_space=pltpu.VMEM)
    dma = pltpu.SemaphoreType.DMA
    arrived = (picked.shape[1], n) + picked.shape[2:]
    return pl.pallas_call(
        functools.partial(share_kernel, width_y),
        out_shape=(
            jax.ShapeDtypeStruct(strain.shape, strain.dtype),
            jax.ShapeDtypeStruct(arrived, picked.dtype),
        ),
        in_specs=[pl.BlockSpec(memory_space=pltpu.SMEM), vmem, vmem],
        out_specs=(vmem, vmem),
        scratch_shapes=[
            pltpu.VMEM((planes, high // 2, wide), strain.dtype),
            pltpu.VMEM((chips - 1, 2, subs, prow, pcol), strain.dtype),
            pltpu.VMEM((2, subs, prow, pcol), strain.dtype),
            dma((chips, 2)), dma((chips, 2)),
            dma((chips - 1, 2, subs)), dma((chips - 1, 2, subs)),
            dma((chips - 1, 2, subs)), dma((chips - 1, 2, subs)),
            dma((chips, 2, subs)), dma((chips, 2, subs)),
            dma((n,)), dma((n,)), dma,
            dma((max(1, groups - 1), n)), dma((max(1, groups - 1), n)),
        ],
        compiler_params=pltpu.CompilerParams(
            collective_id=0, has_side_effects=True, vmem_limit_bytes=40 * 1024 * 1024
        ),
        name="share",
    )(flags, strain, picked)


def body(width_y, strain_slots, templates, cutoffs, lists, owner, slides):
    devices = lax.axis_size("tpl")
    own_index = lax.axis_index("tpl")
    per_device = lists.shape[1]
    chosen = lists.reshape(-1)
    dets = strain_slots.shape[1]
    strain = strain_slots[0].reshape(dets * 2, FOLD, WIDE)
    flags = jnp.stack([own_index == owner[0], own_index // 2 == owner[0] // 2]).astype(jnp.int32)
    rows = templates.shape[2] // WIDE
    picked = templates.reshape(-1, 2, rows, WIDE)[chosen]
    picked = picked.reshape(devices, per_device * 2, rows, WIDE)
    strain, arrived = run_share(width_y, flags, strain, picked)
    strain = strain.reshape(dets, 2, FOLD, WIDE)
    arrived = arrived.reshape(per_device, 2, devices, rows, WIDE)
    own_ids = lax.dynamic_index_in_dim(lists, own_index, 0, keepdims=False)
    row_phase, col_phase = phases(slides)
    return run_filter(cutoffs[own_ids], strain, arrived, row_phase, col_phase)


def solution(mesh):
    in_specs = (
        P(("grp", "tpl"), None, None, None),
        P(None, None, "tpl"),
        P(),
        P(),
        P("grp"),
        P("grp"),
    )
    out_specs = (P(("grp", "tpl")), P(("grp", "tpl")))
    width_y = len({d.coords[1] for d in mesh.devices[0].flat})
    return jax.shard_map(functools.partial(body, width_y), mesh=mesh, in_specs=in_specs, out_specs=out_specs, check_vma=False)
```

```python
import functools

import jax
import jax.numpy as jnp
import numpy as np
from jax import lax
from jax.experimental import pallas as pl
from jax.experimental.pallas import tpu as pltpu
from jax.sharding import PartitionSpec as P

ROWS = 512
COLS = 512
RADIX = 4
FOLD = ROWS // RADIX
WIDE = RADIX * COLS
HALF = COLS // 2

two_pi = 6.283185307179586
eps_norm = 1e-06


def turn_table(left_ids, right_ids, period):
    product_idx = left_ids[:, None] * right_ids[None, :] % period
    angles = product_idx.astype(np.float32) * np.float32(two_pi / period)
    return np.cos(angles), np.sin(angles)


def constant_tables():
    ids = np.arange(ROWS, dtype=np.int32)
    cos, sin = turn_table(ids[:FOLD], ids, ROWS)
    first = []
    for r in range(RADIX):
        c, s = cos[:, r::RADIX], sin[:, r::RADIX]
        first.append(np.concatenate([np.concatenate([c, -s], 1), np.concatenate([s, c], 1)], 0))
    twiddle = np.stack(turn_table(ids, ids, ROWS * COLS))
    cos, sin = turn_table(ids, ids[: HALF + 1], COLS)
    sin = sin[:, :HALF].copy()
    sin[:, 0] = cos[:, HALF]
    second = np.concatenate([cos[:, :HALF], sin], 1)
    return np.stack(first).astype(jnp.bfloat16), twiddle, second.astype(jnp.bfloat16)


def filter_kernel(
    cutoffs, strain, wave, row_phase, col_phase, first, twiddle, second,
    peaks, norms, turned, masked, twisted, total_q, total_r,
):
    dets = strain.shape[0]
    templates = wave.shape[0]
    bins = ROWS * COLS

    def turn(i, _):
        d, rows = i // 8, pl.ds(pl.multiple_of(i % 8 * 16, 16), 16)
        for c in range(WIDE // 512):
            cols = pl.ds(c * 512, 512)
            rr = jnp.concatenate([row_phase[d, 0, rows, :]] * 4, 1)
            ri = jnp.concatenate([row_phase[d, 1, rows, :]] * 4, 1)
            cr, ci = col_phase[d, 0, :, cols], col_phase[d, 1, :, cols]
            pr, pi = rr * cr - ri * ci, rr * ci + ri * cr
            xr = strain[d, 0, rows, cols].astype(jnp.float32)
            xi = strain[d, 1, rows, cols].astype(jnp.float32)
            turned[d, 0, rows, cols] = xr * pr - xi * pi
            turned[d, 1, rows, cols] = xr * pi + xi * pr
        return 0

    lax.fori_loop(0, dets * 8, turn, 0)

    def one_template(t, _):
        cutoff = cutoffs[t]

        blocks = 8 // wave.shape[3]

        def mask(i, acc):
            rows = pl.ds(pl.multiple_of(i * 8, 8), 8)
            for c in range(WIDE // 512):
                cols = pl.ds(c * 512, 512)
                at = (
                    lax.broadcasted_iota(jnp.int32, (8, 512), 0) + i * 8
                ) * WIDE + lax.broadcasted_iota(jnp.int32, (8, 512), 1) + c * 512
                inside = at < cutoff
                parts = []
                for p in range(2):
                    got = [
                        wave[t, p, i * blocks + e, :, cols].astype(jnp.float32) for e in range(blocks)
                    ]
                    got = got[0] if blocks == 1 else jnp.concatenate(got, 0)
                    parts.append(jnp.where(inside, got, 0.0))
                    masked[p, rows, cols] = parts[p]
                acc = acc + (parts[0] * parts[0] + parts[1] * parts[1])
            return acc

        acc = lax.fori_loop(0, FOLD // 8, mask, jnp.zeros((8, 512), jnp.float32))
        sigmasq = jnp.sum(acc)

        def one_detector(d, _):
            for c in range(COLS // 256):
                parts = []
                for r in range(RADIX):
                    cols = pl.ds(r * COLS + c * 256, 256)
                    xr, xi = turned[d, 0, :, cols], turned[d, 1, :, cols]
                    wr, wi = masked[0, :, cols], masked[1, :, cols]
                    product = jnp.concatenate([xr * wr + xi * wi, xi * wr - xr * wi], 0)
                    out = jnp.dot(
                        first[r], product.astype(jnp.bfloat16), preferred_element_type=jnp.float32
                    )
                    parts.append((out[:FOLD], out[FOLD:]))
                (r0, i0), (r1, i1), (r2, i2), (r3, i3) = parts
                ar, ai, br, bi = r0 + r2, i0 + i2, r0 - r2, i0 - i2
                cr, ci, dr, di = r1 + r3, i1 + i3, i3 - i1, r1 - r3
                sections = (
                    (ar + cr, ai + ci), (br + dr, bi + di), (ar - cr, ai - ci), (br - dr, bi - di)
                )
                cols = pl.ds(c * 256, 256)
                for q, (sr, si) in enumerate(sections):
                    rows = pl.ds(q * FOLD, FOLD)
                    tc, ts = twiddle[0, rows, cols], twiddle[1, rows, cols]
                    twisted[0, rows, cols] = (sr * tc - si * ts).astype(jnp.bfloat16)
                    twisted[1, rows, cols] = (sr * ts + si * tc).astype(jnp.bfloat16)
            for q in range(RADIX):
                rows = pl.ds(q * FOLD, FOLD)
                ac = jnp.dot(twisted[0, rows, :], second[...], preferred_element_type=jnp.float32)
                db = jnp.dot(twisted[1, rows, :], second[...], preferred_element_type=jnp.float32)
                a, c, dd, b = ac[:, :HALF], ac[:, HALF:], db[:, :HALF], db[:, HALF:]
                ad, bc = a * a + dd * dd, b * b + c * c
                both = ad + bc
                cross = 2.0 * (c * dd - a * b)
                lane = lax.broadcasted_iota(jnp.int32, both.shape, 1)
                edge = lane == 0
                both, cross = jnp.where(edge, 0.5 * both, both), jnp.where(edge, 0.5 * (ad - bc), cross)

                @pl.when(d == 0)
                def _():
                    total_q[rows, :] = both
                    total_r[rows, :] = cross

                @pl.when(d > 0)
                def _():
                    total_q[rows, :] += both
                    total_r[rows, :] += cross
            return 0

        lax.fori_loop(0, dets, one_detector, 0)

        def largest(i, acc):
            rows = pl.ds(pl.multiple_of(i * 32, 32), 32)
            return jnp.maximum(acc, total_q[rows, :] + jnp.abs(total_r[rows, :]))

        best = lax.fori_loop(0, ROWS // 32, largest, jnp.zeros((32, HALF), jnp.float32))
        peaks[t] = jnp.max(best) / (2.0 * (sigmasq + eps_norm))
        norms[t] = sigmasq / bins
        return 0

    lax.fori_loop(0, templates, one_template, 0)


def run_filter(cutoffs, strain, wave, row_phase, col_phase):
    templates, dets = wave.shape[0], strain.shape[0]
    first, twiddle, second = constant_tables()
    vmem = pl.BlockSpec(memory_space=pltpu.VMEM)
    smem = pl.BlockSpec(memory_space=pltpu.SMEM)
    out = jax.ShapeDtypeStruct((templates,), jnp.float32)
    return pl.pallas_call(
        filter_kernel,
        out_shape=(out, out),
        in_specs=[smem] + [vmem] * 7,
        out_specs=(smem, smem),
        scratch_shapes=[
            pltpu.VMEM((dets, 2, FOLD, WIDE), jnp.float32),
            pltpu.VMEM((2, FOLD, WIDE), jnp.float32),
            pltpu.VMEM((2, ROWS, COLS), jnp.bfloat16),
            pltpu.VMEM((ROWS, HALF), jnp.float32),
            pltpu.VMEM((ROWS, HALF), jnp.float32),
        ],
        compiler_params=pltpu.CompilerParams(vmem_limit_bytes=30 * 1024 * 1024),
        name="filter",
    )(cutoffs, strain, wave, row_phase, col_phase, jnp.asarray(first), jnp.asarray(twiddle), jnp.asarray(second))


def phases(slides):
    total = ROWS * COLS
    slides = slides[:, None]
    row = jnp.arange(FOLD, dtype=jnp.int32)[None] * slides % FOLD
    col = jnp.arange(WIDE, dtype=jnp.int32)[None] * slides % total
    row = row.astype(jnp.float32) * (two_pi / FOLD)
    col = col.astype(jnp.float32) * (two_pi / total)
    row = jnp.stack([jnp.cos(row), jnp.sin(row)], 1)
    col = jnp.stack([jnp.cos(col), jnp.sin(col)], 1)
    return jnp.broadcast_to(row[..., None], row.shape + (128,)), col[:, :, None, :]


MESH = pl.DeviceIdType.MESH


def share_kernel(
    width_y, flags, chosen, strain, bank, full, arrived, picked, other, ring_in, first_out,
    core_send, core_recv, sum_send, sum_recv, all_send, all_recv, part_send, part_recv,
    swap_send, swap_recv, own_sem, cross_send, cross_recv,
):
    n, groups = lax.axis_size("tpl"), lax.axis_size("grp")
    me, group = lax.axis_index("tpl"), lax.axis_index("grp")
    chips = n // 2
    core, chip = me % 2, me // 2
    depth = chips // width_y
    y, z = chip % width_y, chip // width_y
    pos = z + y * (2 * depth - 1 - 2 * z)
    half = strain.shape[1] // 2
    prow, pcol = ring_in.shape[3], ring_in.shape[4]
    colparts = strain.shape[2] // pcol
    subs = strain.shape[0] // 2
    share = arrived.shape[0] // groups
    mine = pl.ds(group * share, share)
    partner = me + 1 - 2 * core

    def device_at(p):
        p = (p + chips) % chips
        yy = p // depth
        zz = p + yy * (2 * depth - 1 - 2 * p)
        return (zz * width_y + yy) * 2 + core

    nexts = (device_at(pos + 1), device_at(pos - 1))

    def chunk(direction, back):
        return (pos - back + 2 * chips) % chips if direction == 0 else (pos + back) % chips

    def spot(base, j):
        rows = pl.multiple_of(base + j // colparts * prow, prow)
        return pl.ds(rows, prow), pl.ds(pl.multiple_of(j % colparts * pcol, pcol), pcol)

    def piece(ref, base, direction, k, j):
        return ref.at[(direction * subs + k,) + spot(base, j)]

    def remote(src, dst, send, recv, **where):
        return pltpu.make_async_remote_copy(
            src_ref=src, dst_ref=dst, send_sem=send, recv_sem=recv,
            device_id=where, device_id_type=MESH,
        )

    def core_copy(direction, back):
        j = chunk(direction, back)
        planes = pl.ds(direction * subs, subs)
        return remote(
            strain.at[(planes,) + spot((1 - core) * half, j)],
            other.at[(planes,) + spot(0, j)],
            core_send.at[back, direction], core_recv.at[back, direction], tpl=partner,
        )

    def sum_copy(direction, k, s):
        src = first_out.at[direction, k]
        if not isinstance(s, int):
            src = ring_in.at[s - 1, direction, k]
        return remote(
            src, ring_in.at[s, direction, k],
            sum_send.at[s, direction, k], sum_recv.at[s, direction, k], tpl=nexts[direction],
        )

    def all_copy(direction, k, s):
        at = piece(full, core * half, direction, k, chunk(direction, s))
        return remote(
            at, at, all_send.at[s, direction, k], all_recv.at[s, direction, k], tpl=nexts[direction]
        )

    def part_copy(direction, k, s, base):
        at = piece(full, base, direction, k, chunk(direction, s))
        return remote(
            at, at, part_send.at[s, direction, k], part_recv.at[s, direction, k], tpl=partner
        )

    def swap_copy(i):
        to = (me - i + n) % n
        return remote(
            picked.at[to, mine], arrived.at[mine, me], swap_send.at[i], swap_recv.at[i], tpl=to
        )

    def swap_arrival(i):
        source = (me + i) % n
        return remote(
            picked.at[me, mine], arrived.at[mine, source], swap_send.at[i], swap_recv.at[i], tpl=source
        )

    def cross_copy(i, g):
        at = arrived.at[mine, (me + i) % n]
        return remote(
            at, at, cross_send.at[g - 1, i], cross_recv.at[g - 1, i], grp=(group + g) % groups
        )

    def cross_arrival(i, g):
        source = (group - g + groups) % groups
        at = arrived.at[pl.ds(source * share, share), (me + i) % n]
        return remote(at, at, cross_send.at[g - 1, i], cross_recv.at[g - 1, i], grp=source)

    barrier = pltpu.get_barrier_semaphore()

    def greet(i, _):
        pl.semaphore_signal(barrier, inc=1, device_id={"tpl": (me + i) % n}, device_id_type=MESH)
        return 0

    lax.fori_loop(1, n, greet, 0)
    for g in range(1, groups):
        pl.semaphore_signal(
            barrier, inc=1, device_id={"grp": (group + g) % groups}, device_id_type=MESH
        )
    pl.semaphore_wait(barrier, n - 1 + groups - 1)

    def start_core(i, _):
        for direction in range(2):
            core_copy(direction, i + 1 - (i + 1) // chips * chips).start()
        return 0

    lax.fori_loop(0, chips, start_core, 0)
    i_own, chip_owns = flags[0], flags[1]
    slots = picked.shape[1] // 2

    def gather(i, _):
        for e in range(slots):
            picked[i, pl.ds(2 * e, 2)] = bank[chosen[i * slots + e]]
        return 0

    lax.fori_loop(0, n, gather, 0)
    own = pltpu.make_async_copy(picked.at[me], arrived.at[:, me], own_sem)
    own.start()
    per_step = -(-(n - 1) // (chips - 3))

    def cross_start(i):
        swap_arrival(i).wait_recv()
        for g in range(1, groups):
            cross_copy(i, g).start()

    def templates_on(step):
        for e in range(per_step):
            at = 1 + step * per_step + e

            @pl.when(at < n)
            def _():
                swap_copy(at).start()

        for e in range(2):
            late = 1 + (step - 3) * 2 + e

            @pl.when((late >= 1) & (late < n))
            def _():
                cross_start(late)

    def candidate(direction, k, j):
        here = piece(strain, core * half, direction, k, j)[...]
        there = piece(other, 0, direction, k, j)[...]
        return jnp.where(i_own != 0, here, there)

    for direction in range(2):
        core_copy(direction, 1).wait_recv()
        for k in range(subs):
            first_out[direction, k] = candidate(direction, k, chunk(direction, 1))
            sum_copy(direction, k, 0).start()

    def joined(direction, k, s, j):
        remote(
            first_out.at[direction, k], ring_in.at[s, direction, k],
            sum_send.at[s, direction, k], sum_recv.at[s, direction, k], tpl=nexts[direction],
        ).wait_recv()
        return jnp.where(chip_owns != 0, candidate(direction, k, j), ring_in[s, direction, k])

    def sum_step(s, _):
        for direction in range(2):
            core_copy(direction, s + 2).wait_recv()
        for k in range(subs):
            for direction in range(2):
                ring_in[s, direction, k] = joined(direction, k, s, chunk(direction, s + 2))
                sum_copy(direction, k, s + 1).start()
        templates_on(s)
        return 0

    lax.fori_loop(0, chips - 2, sum_step, 0)
    for direction in range(2):
        core_copy(direction, 0).wait_recv()
    for k in range(subs):
        for direction in range(2):
            piece(full, core * half, direction, k, pos)[...] = joined(direction, k, chips - 2, pos)
            all_copy(direction, k, 0).start()
            part_copy(direction, k, 0, core * half).start()

    def all_step(s, _):
        for k in range(subs):
            for direction in range(2):
                at = piece(full, core * half, direction, k, chunk(direction, s + 1))
                remote(
                    at, at, all_send.at[s, direction, k], all_recv.at[s, direction, k],
                    tpl=nexts[direction],
                ).wait_recv()
                all_copy(direction, k, s + 1).start()
                part_copy(direction, k, s + 1, core * half).start()
        templates_on(chips - 2 + s)
        return 0

    lax.fori_loop(0, chips - 2, all_step, 0)
    last = chips - 2
    for k in range(subs):
        for direction in range(2):
            at = piece(full, core * half, direction, k, chunk(direction, last + 1))
            remote(
                at, at, all_send.at[last, direction, k], all_recv.at[last, direction, k],
                tpl=nexts[direction],
            ).wait_recv()
            part_copy(direction, k, last + 1, core * half).start()

    def finish(s, _):
        for direction in range(2):
            core_copy(direction, s).wait_send()
            for k in range(subs):
                part_copy(direction, k, s, core * half).wait_send()
                part_copy(direction, k, s, (1 - core) * half).wait_recv()
        return 0

    lax.fori_loop(0, chips, finish, 0)

    def finish_ring(s, _):
        for direction in range(2):
            for k in range(subs):
                all_copy(direction, k, s).wait_send()
                remote(
                    first_out.at[direction, k], ring_in.at[s, direction, k],
                    sum_send.at[s, direction, k], sum_recv.at[s, direction, k], tpl=nexts[direction],
                ).wait_send()
        return 0

    lax.fori_loop(0, chips - 1, finish_ring, 0)

    def finish_swap(i, _):
        swap_copy(i).wait_send()
        for g in range(1, groups):
            cross_copy(i, g).wait_send()
            cross_arrival(i, g).wait_recv()
        return 0

    lax.fori_loop(1, n, finish_swap, 0)
    own.wait()


def run_share(width_y, flags, chosen, strain, bank):
    n, groups = lax.axis_size("tpl"), lax.axis_size("grp")
    chips = n // 2
    planes, high, wide = strain.shape
    subs = planes // 2
    rowparts = max(1, chips * 256 // wide)
    prow, pcol = high // 2 // rowparts, wide * rowparts // chips
    vmem = pl.BlockSpec(memory_space=pltpu.VMEM)
    dma = pltpu.SemaphoreType.DMA
    pieces = chosen.shape[0] // n * 2
    arrived = (pieces, n) + bank.shape[2:]
    return pl.pallas_call(
        functools.partial(share_kernel, width_y),
        out_shape=(
            jax.ShapeDtypeStruct(strain.shape, strain.dtype),
            jax.ShapeDtypeStruct(arrived, bank.dtype),
        ),
        in_specs=[pl.BlockSpec(memory_space=pltpu.SMEM)] * 2 + [vmem, vmem],
        out_specs=(vmem, vmem),
        scratch_shapes=[
            pltpu.VMEM((n, pieces) + bank.shape[2:], bank.dtype),
            pltpu.VMEM((planes, high // 2, wide), strain.dtype),
            pltpu.VMEM((chips - 1, 2, subs, prow, pcol), strain.dtype),
            pltpu.VMEM((2, subs, prow, pcol), strain.dtype),
            dma((chips, 2)), dma((chips, 2)),
            dma((chips - 1, 2, subs)), dma((chips - 1, 2, subs)),
            dma((chips - 1, 2, subs)), dma((chips - 1, 2, subs)),
            dma((chips, 2, subs)), dma((chips, 2, subs)),
            dma((n,)), dma((n,)), dma,
            dma((max(1, groups - 1), n)), dma((max(1, groups - 1), n)),
        ],
        compiler_params=pltpu.CompilerParams(
            collective_id=0, has_side_effects=True, vmem_limit_bytes=22 * 1024 * 1024
        ),
        name="share",
    )(flags, chosen, strain, bank)


def body(width_y, strain_slots, templates, cutoffs, lists, owner, slides):
    devices = lax.axis_size("tpl")
    own_index = lax.axis_index("tpl")
    per_device = lists.shape[1]
    chosen = lists.reshape(-1)
    dets = strain_slots.shape[1]
    strain = strain_slots[0].reshape(dets * 2, FOLD, WIDE)
    flags = jnp.stack([own_index == owner[0], own_index // 2 == owner[0] // 2]).astype(jnp.int32)
    rows = templates.shape[2] // WIDE
    bank = templates.reshape(-1, 2, rows, WIDE)
    strain, arrived = run_share(width_y, flags, chosen, strain, bank)
    strain = strain.reshape(dets, 2, FOLD, WIDE)
    arrived = arrived.reshape(per_device, 2, devices, rows, WIDE)
    own_ids = lax.dynamic_index_in_dim(lists, own_index, 0, keepdims=False)
    row_phase, col_phase = phases(slides)
    return run_filter(cutoffs[own_ids], strain, arrived, row_phase, col_phase)


def solution(mesh):
    in_specs = (
        P(("grp", "tpl"), None, None, None),
        P(None, None, "tpl"),
        P(),
        P(),
        P("grp"),
        P("grp"),
    )
    out_specs = (P(("grp", "tpl")), P(("grp", "tpl")))
    width_y = len({d.coords[1] for d in mesh.devices[0].flat})
    return jax.shard_map(functools.partial(body, width_y), mesh=mesh, in_specs=in_specs, out_specs=out_specs, check_vma=False)
```

```python
import functools

import jax
import jax.numpy as jnp
import numpy as np
from jax import lax
from jax.experimental import pallas as pl
from jax.experimental.pallas import tpu as pltpu
from jax.sharding import PartitionSpec as P

ROWS = 512
COLS = 512
RADIX = 4
FOLD = ROWS // RADIX
WIDE = RADIX * COLS
HALF = COLS // 2

two_pi = 6.283185307179586
eps_norm = 1e-06


def turn_table(left_ids, right_ids, period):
    product_idx = left_ids[:, None] * right_ids[None, :] % period
    angles = product_idx.astype(np.float32) * np.float32(two_pi / period)
    return np.cos(angles), np.sin(angles)


def constant_tables():
    ids = np.arange(ROWS, dtype=np.int32)
    cos, sin = turn_table(ids[:FOLD], ids, ROWS)
    first = []
    for r in range(RADIX):
        c, s = cos[:, r::RADIX], sin[:, r::RADIX]
        first.append(np.concatenate([np.concatenate([c, -s], 1), np.concatenate([s, c], 1)], 0))
    twiddle = np.stack(turn_table(ids, ids, ROWS * COLS))
    cos, sin = turn_table(ids, ids[: HALF + 1], COLS)
    sin = sin[:, :HALF].copy()
    sin[:, 0] = cos[:, HALF]
    second = np.concatenate([cos[:, :HALF], sin], 1)
    return np.stack(first).astype(jnp.bfloat16), twiddle, second.astype(jnp.bfloat16)


def filter_kernel(
    cutoffs, strain, wave, row_phase, col_phase, first, twiddle, second,
    peaks, norms, turned, masked, twisted, total_q, total_r,
):
    dets = strain.shape[0]
    templates = wave.shape[0]
    bins = ROWS * COLS

    def turn(i, _):
        d, rows = i // 8, pl.ds(pl.multiple_of(i % 8 * 16, 16), 16)
        for c in range(WIDE // 512):
            cols = pl.ds(c * 512, 512)
            rr = jnp.concatenate([row_phase[d, 0, rows, :]] * 4, 1)
            ri = jnp.concatenate([row_phase[d, 1, rows, :]] * 4, 1)
            cr, ci = col_phase[d, 0, :, cols], col_phase[d, 1, :, cols]
            pr, pi = rr * cr - ri * ci, rr * ci + ri * cr
            xr = strain[d, 0, rows, cols].astype(jnp.float32)
            xi = strain[d, 1, rows, cols].astype(jnp.float32)
            turned[d, 0, rows, cols] = xr * pr - xi * pi
            turned[d, 1, rows, cols] = xr * pi + xi * pr
        return 0

    lax.fori_loop(0, dets * 8, turn, 0)

    def one_template(t, _):
        cutoff = cutoffs[t]

        blocks = 8 // wave.shape[3]

        def mask(i, acc):
            rows = pl.ds(pl.multiple_of(i * 8, 8), 8)
            for c in range(WIDE // 512):
                cols = pl.ds(c * 512, 512)
                at = (
                    lax.broadcasted_iota(jnp.int32, (8, 512), 0) + i * 8
                ) * WIDE + lax.broadcasted_iota(jnp.int32, (8, 512), 1) + c * 512
                inside = at < cutoff
                parts = []
                for p in range(2):
                    got = [
                        wave[t, p, i * blocks + e, :, cols].astype(jnp.float32) for e in range(blocks)
                    ]
                    got = got[0] if blocks == 1 else jnp.concatenate(got, 0)
                    parts.append(jnp.where(inside, got, 0.0))
                    masked[p, rows, cols] = parts[p]
                acc = acc + (parts[0] * parts[0] + parts[1] * parts[1])
            return acc

        acc = lax.fori_loop(0, FOLD // 8, mask, jnp.zeros((8, 512), jnp.float32))
        sigmasq = jnp.sum(acc)

        def one_detector(d, _):
            for c in range(COLS // 256):
                parts = []
                for r in range(RADIX):
                    cols = pl.ds(r * COLS + c * 256, 256)
                    xr, xi = turned[d, 0, :, cols], turned[d, 1, :, cols]
                    wr, wi = masked[0, :, cols], masked[1, :, cols]
                    product = jnp.concatenate([xr * wr + xi * wi, xi * wr - xr * wi], 0)
                    out = jnp.dot(
                        first[r], product.astype(jnp.bfloat16), preferred_element_type=jnp.float32
                    )
                    parts.append((out[:FOLD], out[FOLD:]))
                (r0, i0), (r1, i1), (r2, i2), (r3, i3) = parts
                ar, ai, br, bi = r0 + r2, i0 + i2, r0 - r2, i0 - i2
                cr, ci, dr, di = r1 + r3, i1 + i3, i3 - i1, r1 - r3
                sections = (
                    (ar + cr, ai + ci), (br + dr, bi + di), (ar - cr, ai - ci), (br - dr, bi - di)
                )
                cols = pl.ds(c * 256, 256)
                for q, (sr, si) in enumerate(sections):
                    rows = pl.ds(q * FOLD, FOLD)
                    tc, ts = twiddle[0, rows, cols], twiddle[1, rows, cols]
                    twisted[0, rows, cols] = (sr * tc - si * ts).astype(jnp.bfloat16)
                    twisted[1, rows, cols] = (sr * ts + si * tc).astype(jnp.bfloat16)
            for q in range(RADIX):
                rows = pl.ds(q * FOLD, FOLD)
                ac = jnp.dot(twisted[0, rows, :], second[...], preferred_element_type=jnp.float32)
                db = jnp.dot(twisted[1, rows, :], second[...], preferred_element_type=jnp.float32)
                a, c, dd, b = ac[:, :HALF], ac[:, HALF:], db[:, :HALF], db[:, HALF:]
                ad, bc = a * a + dd * dd, b * b + c * c
                both = ad + bc
                cross = 2.0 * (c * dd - a * b)
                lane = lax.broadcasted_iota(jnp.int32, both.shape, 1)
                edge = lane == 0
                both, cross = jnp.where(edge, 0.5 * both, both), jnp.where(edge, 0.5 * (ad - bc), cross)

                @pl.when(d == 0)
                def _():
                    total_q[rows, :] = both
                    total_r[rows, :] = cross

                @pl.when(d > 0)
                def _():
                    total_q[rows, :] += both
                    total_r[rows, :] += cross
            return 0

        lax.fori_loop(0, dets, one_detector, 0)

        def largest(i, acc):
            rows = pl.ds(pl.multiple_of(i * 32, 32), 32)
            return jnp.maximum(acc, total_q[rows, :] + jnp.abs(total_r[rows, :]))

        best = lax.fori_loop(0, ROWS // 32, largest, jnp.zeros((32, HALF), jnp.float32))
        peaks[t] = jnp.max(best) / (2.0 * (sigmasq + eps_norm))
        norms[t] = sigmasq / bins
        return 0

    lax.fori_loop(0, templates, one_template, 0)


def run_filter(cutoffs, strain, wave, row_phase, col_phase):
    templates, dets = wave.shape[0], strain.shape[0]
    first, twiddle, second = constant_tables()
    vmem = pl.BlockSpec(memory_space=pltpu.VMEM)
    smem = pl.BlockSpec(memory_space=pltpu.SMEM)
    out = jax.ShapeDtypeStruct((templates,), jnp.float32)
    return pl.pallas_call(
        filter_kernel,
        out_shape=(out, out),
        in_specs=[smem] + [vmem] * 7,
        out_specs=(smem, smem),
        scratch_shapes=[
            pltpu.VMEM((dets, 2, FOLD, WIDE), jnp.float32),
            pltpu.VMEM((2, FOLD, WIDE), jnp.float32),
            pltpu.VMEM((2, ROWS, COLS), jnp.bfloat16),
            pltpu.VMEM((ROWS, HALF), jnp.float32),
            pltpu.VMEM((ROWS, HALF), jnp.float32),
        ],
        compiler_params=pltpu.CompilerParams(vmem_limit_bytes=30 * 1024 * 1024),
        name="filter",
    )(cutoffs, strain, wave, row_phase, col_phase, jnp.asarray(first), jnp.asarray(twiddle), jnp.asarray(second))


def phases(slides):
    total = ROWS * COLS
    slides = slides[:, None]
    row = jnp.arange(FOLD, dtype=jnp.int32)[None] * slides % FOLD
    col = jnp.arange(WIDE, dtype=jnp.int32)[None] * slides % total
    row = row.astype(jnp.float32) * (two_pi / FOLD)
    col = col.astype(jnp.float32) * (two_pi / total)
    row = jnp.stack([jnp.cos(row), jnp.sin(row)], 1)
    col = jnp.stack([jnp.cos(col), jnp.sin(col)], 1)
    return jnp.broadcast_to(row[..., None], row.shape + (128,)), col[:, :, None, :]


MESH = pl.DeviceIdType.MESH


def share_kernel(
    width_y, flags, chosen, strain, bank, full, arrived, picked, other, ring_in, first_out,
    core_send, core_recv, sum_send, sum_recv, all_send, all_recv, part_send, part_recv,
    swap_send, swap_recv, own_sem, cross_send, cross_recv,
):
    n, groups = lax.axis_size("tpl"), lax.axis_size("grp")
    me, group = lax.axis_index("tpl"), lax.axis_index("grp")
    chips = n // 2
    core, chip = me % 2, me // 2
    depth = chips // width_y
    y, z = chip % width_y, chip // width_y
    pos = z + y * (2 * depth - 1 - 2 * z)
    half = strain.shape[1] // 2
    prow, pcol = ring_in.shape[3], ring_in.shape[4]
    colparts = strain.shape[2] // pcol
    subs = strain.shape[0]
    arm = chips // 2
    share = arrived.shape[0] // groups
    mine = pl.ds(group * share, share)
    partner = me + 1 - 2 * core

    def device_at(p):
        p = (p + chips) % chips
        yy = p // depth
        zz = p + yy * (2 * depth - 1 - 2 * p)
        return (zz * width_y + yy) * 2 + core

    nexts = (device_at(pos + 1), device_at(pos - 1))

    def chunk(direction, back):
        return (pos - back + 2 * chips) % chips if direction == 0 else (pos + back) % chips

    def spot(base, j):
        rows = pl.multiple_of(base + j // colparts * prow, prow)
        return pl.ds(rows, prow), pl.ds(pl.multiple_of(j % colparts * pcol, pcol), pcol)

    def piece(ref, base, direction, k, j):
        return ref.at[(k,) + spot(base, j)]

    def remote(src, dst, send, recv, **where):
        return pltpu.make_async_remote_copy(
            src_ref=src, dst_ref=dst, send_sem=send, recv_sem=recv,
            device_id=where, device_id_type=MESH,
        )

    def core_copy(back):
        j = chunk(0, back)
        planes = pl.ds(0, subs)
        return remote(
            strain.at[(planes,) + spot((1 - core) * half, j)],
            other.at[(planes,) + spot(0, j)],
            core_send.at[back], core_recv.at[back], tpl=partner,
        )

    def covered(direction, k):
        return (k < subs // 2) == (direction == 0)

    def sum_copy(direction, k, s, started=False):
        src = first_out.at[direction, k] if started else ring_in.at[max(s - 1, 0), direction, k]
        return remote(
            src, ring_in.at[s, direction, k],
            sum_send.at[s, direction, k], sum_recv.at[s, direction, k], tpl=nexts[direction],
        )

    def all_copy(direction, k, s):
        at = piece(full, core * half, direction, k, chunk(direction, s))
        return remote(
            at, at, all_send.at[s, direction, k], all_recv.at[s, direction, k], tpl=nexts[direction]
        )

    def part_copy(direction, k, s, base):
        at = piece(full, base, direction, k, chunk(direction, s))
        return remote(
            at, at, part_send.at[s, direction, k], part_recv.at[s, direction, k], tpl=partner
        )

    def swap_copy(i):
        to = (me - i + n) % n
        return remote(
            picked.at[to, mine], arrived.at[mine, me], swap_send.at[i], swap_recv.at[i], tpl=to
        )

    def swap_arrival(i):
        source = (me + i) % n
        return remote(
            picked.at[me, mine], arrived.at[mine, source], swap_send.at[i], swap_recv.at[i], tpl=source
        )

    def cross_copy(i, g):
        at = arrived.at[mine, (me + i) % n]
        return remote(
            at, at, cross_send.at[g - 1, i], cross_recv.at[g - 1, i], grp=(group + g) % groups
        )

    def cross_arrival(i, g):
        source = (group - g + groups) % groups
        at = arrived.at[pl.ds(source * share, share), (me + i) % n]
        return remote(at, at, cross_send.at[g - 1, i], cross_recv.at[g - 1, i], grp=source)

    barrier = pltpu.get_barrier_semaphore()

    def greet(i, _):
        pl.semaphore_signal(barrier, inc=1, device_id={"tpl": (me + i) % n}, device_id_type=MESH)
        return 0

    lax.fori_loop(1, n, greet, 0)
    for g in range(1, groups):
        pl.semaphore_signal(
            barrier, inc=1, device_id={"grp": (group + g) % groups}, device_id_type=MESH
        )
    pl.semaphore_wait(barrier, n - 1 + groups - 1)

    order = [arm]
    for h in range(arm - 1, 0, -1):
        order += [h, chips - h]
    order.append(0)
    for back in order:
        core_copy(back).start()
    i_own, chip_owns, from_left = flags[0], flags[1], flags[2]
    slots = picked.shape[1] // 2

    def gather(i, _):
        for e in range(slots):
            picked[i, pl.ds(2 * e, 2)] = bank[chosen[i * slots + e]]
        return 0

    lax.fori_loop(0, n, gather, 0)
    own = pltpu.make_async_copy(picked.at[me], arrived.at[:, me], own_sem)
    own.start()
    per_step = -(-(n - 1) // (arm - 1))
    late_step = -(-(n - 1) // (2 * arm - 3))

    def cross_start(i):
        swap_arrival(i).wait_recv()
        for g in range(1, groups):
            cross_copy(i, g).start()

    def templates_on(step):
        for at in range(1 + step * per_step, min(n, 1 + (step + 1) * per_step)):
            swap_copy(at).start()
        late = 1 + (step - 2) * late_step
        for at in range(max(late, 1), min(n, late + late_step)):
            cross_start(at)

    def candidate(direction, k, j):
        here = piece(strain, core * half, direction, k, j)[...]
        there = piece(other, 0, direction, k, j)[...]
        return jnp.where(i_own != 0, here, there)

    core_copy(arm).wait_recv()
    for k in range(subs):
        direction = 0 if covered(0, k) else 1
        first_out[direction, k] = candidate(direction, k, chunk(1, arm))
        sum_copy(direction, k, 0, True).start()
    for back in (arm - 1, chips - arm + 1):
        core_copy(back).wait_recv()
    for k in range(subs):
        direction = 1 if covered(0, k) else 0
        first_out[direction, k] = candidate(direction, k, chunk(1 - direction, arm - 1))
        sum_copy(direction, k, 1, True).start()
    for s in range(arm - 1):
        h = arm - 1 - s
        if s > 0:
            for back in (h, chips - h):
                core_copy(back).wait_recv()
        for k in range(subs):
            for direction in range(2):
                if s > 0 or covered(direction, k):
                    sum_copy(direction, k, s).wait_recv()
                    ring_in[s, direction, k] = jnp.where(
                        chip_owns != 0,
                        candidate(direction, k, chunk(1 - direction, h)),
                        ring_in[s, direction, k],
                    )
                    sum_copy(direction, k, s + 1).start()
        templates_on(s)
    core_copy(0).wait_recv()
    for k in range(subs):
        for direction in range(2):
            sum_copy(direction, k, arm - 1).wait_recv()
        left = from_left + (flags[3] if covered(0, k) else 0)
        best = jnp.where(left != 0, ring_in[arm - 1, 0, k], ring_in[arm - 1, 1, k])
        piece(full, core * half, 0, k, pos)[...] = jnp.where(
            chip_owns != 0, candidate(0, k, pos), best
        )
        for direction in range(2):
            all_copy(direction, k, 0).start()
        part_copy(0, k, 0, core * half).start()
    for s in range(arm):
        for k in range(subs):
            for direction in range(2):
                if s < arm - 1 or covered(direction, k):
                    at = piece(full, core * half, direction, k, chunk(direction, s + 1))
                    remote(
                        at, at, all_send.at[s, direction, k], all_recv.at[s, direction, k],
                        tpl=nexts[direction],
                    ).wait_recv()
                    if s + 1 < arm - 1 or (s + 1 == arm - 1 and covered(direction, k)):
                        all_copy(direction, k, s + 1).start()
                    part_copy(direction, k, s + 1, core * half).start()
        templates_on(arm - 1 + s)
    for back in range(chips):
        core_copy(back).wait_send()
    for s in range(arm + 1):
        for k in range(subs):
            for direction in range(2):
                if (s == 0 and direction == 0) or 0 < s < arm or (s == arm and covered(direction, k)):
                    part_copy(direction, k, s, core * half).wait_send()
                    part_copy(direction, k, s, (1 - core) * half).wait_recv()
                if s < arm - 1 or (s == arm - 1 and covered(direction, k)):
                    all_copy(direction, k, s).wait_send()
                if 0 < s < arm or (s == 0 and covered(direction, k)):
                    sum_copy(direction, k, s).wait_send()

    def finish_swap(i, _):
        swap_copy(i).wait_send()
        for g in range(1, groups):
            cross_copy(i, g).wait_send()
            cross_arrival(i, g).wait_recv()
        return 0

    lax.fori_loop(1, n, finish_swap, 0)
    own.wait()


def run_share(width_y, flags, chosen, strain, bank):
    n, groups = lax.axis_size("tpl"), lax.axis_size("grp")
    chips = n // 2
    planes, high, wide = strain.shape
    subs = planes
    rowparts = max(1, chips * 256 // wide)
    prow, pcol = high // 2 // rowparts, wide * rowparts // chips
    vmem = pl.BlockSpec(memory_space=pltpu.VMEM)
    dma = pltpu.SemaphoreType.DMA
    pieces = chosen.shape[0] // n * 2
    arrived = (pieces, n) + bank.shape[2:]
    return pl.pallas_call(
        functools.partial(share_kernel, width_y),
        out_shape=(
            jax.ShapeDtypeStruct(strain.shape, strain.dtype),
            jax.ShapeDtypeStruct(arrived, bank.dtype),
        ),
        in_specs=[pl.BlockSpec(memory_space=pltpu.SMEM)] * 2 + [vmem, vmem],
        out_specs=(vmem, vmem),
        scratch_shapes=[
            pltpu.VMEM((n, pieces) + bank.shape[2:], bank.dtype),
            pltpu.VMEM((planes, high // 2, wide), strain.dtype),
            pltpu.VMEM((chips // 2, 2, subs, prow, pcol), strain.dtype),
            pltpu.VMEM((2, subs, prow, pcol), strain.dtype),
            dma((chips,)), dma((chips,)),
            dma((chips // 2, 2, subs)), dma((chips // 2, 2, subs)),
            dma((chips // 2, 2, subs)), dma((chips // 2, 2, subs)),
            dma((chips // 2 + 1, 2, subs)), dma((chips // 2 + 1, 2, subs)),
            dma((n,)), dma((n,)), dma,
            dma((max(1, groups - 1), n)), dma((max(1, groups - 1), n)),
        ],
        compiler_params=pltpu.CompilerParams(
            collective_id=0, has_side_effects=True, vmem_limit_bytes=22 * 1024 * 1024
        ),
        name="share",
    )(flags, chosen, strain, bank)


def body(width_y, strain_slots, templates, cutoffs, lists, owner, slides):
    devices = lax.axis_size("tpl")
    own_index = lax.axis_index("tpl")
    per_device = lists.shape[1]
    chosen = lists.reshape(-1)
    dets = strain_slots.shape[1]
    strain = strain_slots[0].reshape(dets * 2, FOLD, WIDE)
    chips = devices // 2
    depth = chips // width_y

    def place(device):
        chip = device // 2
        return chip // width_y + chip % width_y * (2 * depth - 1 - 2 * (chip // width_y))

    ahead = (place(owner[0]) - place(own_index)) % chips
    flags = jnp.stack([own_index == owner[0], ahead == 0, ahead > chips // 2, ahead == chips // 2])
    flags = flags.astype(jnp.int32)
    rows = templates.shape[2] // WIDE
    bank = templates.reshape(-1, 2, rows, WIDE)
    strain, arrived = run_share(width_y, flags, chosen, strain, bank)
    strain = strain.reshape(dets, 2, FOLD, WIDE)
    arrived = arrived.reshape(per_device, 2, devices, rows, WIDE)
    own_ids = lax.dynamic_index_in_dim(lists, own_index, 0, keepdims=False)
    row_phase, col_phase = phases(slides)
    return run_filter(cutoffs[own_ids], strain, arrived, row_phase, col_phase)


def solution(mesh):
    in_specs = (
        P(("grp", "tpl"), None, None, None),
        P(None, None, "tpl"),
        P(),
        P(),
        P("grp"),
        P("grp"),
    )
    out_specs = (P(("grp", "tpl")), P(("grp", "tpl")))
    width_y = len({d.coords[1] for d in mesh.devices[0].flat})
    return jax.shard_map(functools.partial(body, width_y), mesh=mesh, in_specs=in_specs, out_specs=out_specs, check_vma=False)
```
